32 devices in a mesh: tok: 8 (over y, x, core), lat: 4 (over z).
Axes of the slice: x: 2, y: 2, z: 4, core: 2. Of those that a mesh axis runs over, the one named last changes fastest.
Arguments:
- captured: bfloat16 [1024, 16384], P(None, 'tok'), may hold values from -6 to 6
- enc_weight: bfloat16 [16384, 16384], P('tok', 'lat'), may hold values from -0.046875 to 0.046875
- enc_bias: float32 [16384], P('lat'), may hold values from -3 to 3
- dec_weight: bfloat16 [16384, 16384], P('lat', 'tok'), may hold values from -0.1875 to 0.1875
- dec_bias: float32 [16384], P('tok'), may hold values from -1.5 to 1.5
- block_ids: int32 [8, 4, 2], P(None, 'lat'), may hold values from 0 to 31, as said below
- block_counts: int32 [8, 4], P(None, 'lat'), may hold values from 1 to 2, as said below
Outputs:
- enc_grad: bfloat16 [16384, 16384], P('tok', 'lat')
- dec_grad: bfloat16 [16384, 16384], P('lat', 'tok')
The draws below stay inside these ranges and needn't reach their ends.
Inputs may be any that keep to these rules, and one draw needn't show every extreme that they name: block_ids[b, s, k] numbers a latent block within latent shard s; the 2 entries of one token block and shard are distinct, and those with k >= block_counts[b, s] are inactive slots. block_counts[b, s] is how many leading slots of block_ids[b, s] are active; some entry equals 2 in every draw.
All inputs are finite; a program needn't handle non-finite values.
Results may differ from the reference program's by a relative error of at most 0.02.
Values may be sent and summed in bfloat16 or wider, within the bound.
A program may use at most 192 MiB of HBM per device.

```python
import jax
import jax.numpy as jnp
from jax import lax

L = 16384
TB = 128
LB = 128
KS = 2
F = 16384
TOKENS = 1024
NTB = 8
LBD = 32
ACTIVE = 1024
N_LAT = 4


def pick_row(row_key):
    return jax.random.permutation(row_key, LBD)[:KS]


def draw_block_ids(key, part):
    row_keys = jax.random.split(jax.random.fold_in(key, 11), NTB * N_LAT)
    chosen = jax.vmap(pick_row)(row_keys)
    return chosen.reshape(NTB, N_LAT, KS).astype(jnp.int32)


def draw_block_counts(key, part):
    base_key = jax.random.fold_in(key, 23)
    key_level, key_extra, key_row, key_col = jax.random.split(base_key, 4)
    levels = jax.random.randint(key_level, (N_LAT,), 0, KS)
    extra_slots = jax.random.randint(key_extra, (NTB, N_LAT), 0, KS)
    counts = 1 + jnp.minimum(extra_slots, levels[None, :])
    row_at = jax.random.randint(key_row, (), 0, NTB)
    col_at = jax.random.randint(key_col, (), 0, N_LAT)
    return counts.at[row_at, col_at].set(KS).astype(jnp.int32)


def level_of(key, shape, shards, least, high):
    def one(dim, parts):
        heights = jax.random.uniform(jax.random.fold_in(jax.random.fold_in(key, 6), dim), (parts,), jnp.float32, least / len(shards), high / len(shards))
        return jnp.repeat(jnp.exp(heights), shape[dim] // parts).reshape((-1,) + (1,) * (len(shape) - dim - 1))

    loudness = one(*shards[0])
    for cut in shards[1:]:
        loudness = loudness * one(*cut)
    return loudness


def bell_draw(key, shape, deviation, reach, shards=(), kind=jnp.bfloat16):
    level = level_of(key, shape, shards, -0.22, 0.18) if shards else 1.0
    drawn = jax.random.normal(key, shape, jnp.float32) * deviation * level
    return jnp.minimum(jnp.maximum(drawn, -reach), reach).astype(kind)


def setup_inputs(seed: int = 0) -> dict:
    streams_of = jax.random.split(jax.random.key(seed), 8)
    captured = bell_draw(streams_of[0], (TOKENS, F), 1.0, 6.0, ((1, 8),))
    enc_weight = bell_draw(streams_of[1], (F, L), F ** -0.5, 0.046875, ((0, 8), (1, 4)))
    enc_bias = bell_draw(streams_of[2], (L,), 0.5, 3.0, ((0, 4),), jnp.float32)
    dec_weight = bell_draw(streams_of[3], (L, F), ACTIVE ** -0.5, 0.1875, ((0, 4), (1, 8)))
    dec_bias = bell_draw(streams_of[4], (F,), 0.25, 1.5, ((0, 8),), jnp.float32)
    block_ids = draw_block_ids(jax.random.fold_in(streams_of[7], 71), 0)
    block_counts = draw_block_counts(jax.random.fold_in(streams_of[7], 71), 0)
    return dict(captured=captured, enc_weight=enc_weight, enc_bias=enc_bias, dec_weight=dec_weight, dec_bias=dec_bias, block_ids=block_ids, block_counts=block_counts)


SCALE_ERR = 0.0625
PENALTY = 0.05


def reference(captured, enc_weight, enc_bias, dec_weight, dec_bias, block_ids, block_counts):
    features = captured.shape[1]
    all_blocks = captured.shape[0] // TB
    lat_blocks = L // LB
    slots = N_LAT * KS
    enc_cube = enc_weight.reshape(features, lat_blocks, LB)
    dec_cube = dec_weight.reshape(lat_blocks, LB, features)
    bias_cube = enc_bias.reshape(lat_blocks, LB)
    offsets = (jnp.arange(N_LAT, dtype=jnp.int32) * LBD)[:, None]
    rows_all = captured.reshape(all_blocks, TB, features)

    def one_block(inputs):
        rows_in, ids_row, counts_row = inputs
        global_ids = (offsets + ids_row).reshape(slots).astype(jnp.int32)
        enc_tiles = jnp.take(enc_cube, global_ids, axis=1).astype(jnp.float32)
        pre_act = jnp.einsum("tf,fmc->mtc", rows_in.astype(jnp.float32), enc_tiles)
        pre_act = pre_act + jnp.take(bias_cube, global_ids, axis=0)[:, None, :]
        live_slots = (jnp.arange(KS, dtype=jnp.int32)[None, :] < counts_row[:, None]).reshape(slots)
        codes = (jax.nn.softplus(pre_act) * live_slots.astype(jnp.float32)[:, None, None]).astype(jnp.bfloat16)
        dec_tiles = jnp.take(dec_cube, global_ids, axis=0).astype(jnp.float32)
        partial_value = jnp.einsum("lktc,lkcf->ltf", codes.astype(jnp.float32).reshape(N_LAT, KS, TB, LB),
                             dec_tiles.reshape(N_LAT, KS, LB, features))
        partial_value = lax.optimization_barrier(partial_value.astype(jnp.bfloat16)).astype(jnp.float32)
        rebuilt = jnp.sum(partial_value, axis=0)
        err_grad = SCALE_ERR * (rebuilt + dec_bias[None, :] - rows_in.astype(jnp.float32))
        err_half = err_grad.astype(jnp.bfloat16)
        code_grads = jnp.einsum("tf,mcf->mtc", err_half.astype(jnp.float32), dec_tiles)
        pre_grads = ((code_grads + PENALTY) * (1.0 - jnp.exp(-codes.astype(jnp.float32)))).astype(jnp.bfloat16)
        return codes, err_half, pre_grads

    codes, err_half, pre_grads = lax.map(one_block, (rows_all, block_ids, block_counts))
    codes_shard = codes.reshape(all_blocks, N_LAT, KS, TB, LB).transpose(1, 0, 2, 3, 4)
    grads_shard = pre_grads.reshape(all_blocks, N_LAT, KS, TB, LB).transpose(1, 0, 2, 3, 4)
    ids_shard = block_ids.transpose(1, 0, 2)

    def one_shard(inputs):
        shard_codes, shard_grads, shard_ids = inputs

        def step(carry, item):
            dec_acc, enc_acc = carry
            code_tiles, grad_tiles, chosen, rows_in, err_rows = item
            tile_dec = jnp.einsum("ktc,tf->kcf", code_tiles.astype(jnp.float32), err_rows.astype(jnp.float32))
            tile_enc = jnp.einsum("tf,ktc->fkc", rows_in.astype(jnp.float32), grad_tiles.astype(jnp.float32))
            return (dec_acc.at[chosen].add(tile_dec), enc_acc.at[:, chosen].add(tile_enc)), None

        start_acc = (jnp.zeros((LBD, LB, features), jnp.float32), jnp.zeros((features, LBD, LB), jnp.float32))
        (dec_acc, enc_acc), unused = lax.scan(step, start_acc, (shard_codes, shard_grads, shard_ids, rows_all, err_half))
        return (dec_acc.reshape(LBD * LB, features).astype(jnp.bfloat16),
                enc_acc.reshape(features, LBD * LB).astype(jnp.bfloat16))

    dec_parts, enc_parts = lax.map(one_shard, (codes_shard, grads_shard, ids_shard))
    dec_grad = dec_parts.reshape(L, features)
    enc_grad = enc_parts.transpose(1, 0, 2).reshape(features, L)
    return enc_grad, dec_grad
```

```python
import functools

import jax
import jax.numpy as jnp
from jax import lax
from jax.experimental import pallas as pl
from jax.experimental.pallas import tpu as pltpu
from jax.sharding import PartitionSpec as P

TB = 128
LB = 128
KS = 2

SCALE_ERR = 0.0625
PENALTY = 0.05
CHUNK = 16
LAG = 4
F32 = jnp.float32
BF16 = jnp.bfloat16
MESH = pl.DeviceIdType.MESH
VMEM = pltpu.VMEM
BIG = 60 * 1024 * 1024


def dot(a, b, ca, cb):
    return lax.dot_general(a, b, (((ca,), (cb,)), ((), ())), preferred_element_type=F32)


def rows_of(b, size):
    return pl.ds(pl.multiple_of(b * size, size), size)


def pre_kernel(ids, counts, cap_hbm, enc_hbm, bias_ref, pre_ref, bsel_ref, live_ref, cap_v, tiles_v, cap_sem, tile_sem):
    blocks = pre_ref.shape[0]

    def loads(b):
        copies = [pltpu.make_async_copy(cap_hbm.at[rows_of(b, TB)], cap_v.at[rows_of(b, TB)], cap_sem.at[b])]
        for k in range(KS):
            copies.append(pltpu.make_async_copy(
                enc_hbm.at[:, rows_of(ids[k, b], LB)], tiles_v.at[b, :, pl.ds(k * LB, LB)], tile_sem.at[b * KS + k]
            ))
        return copies

    def begin(b, carry):
        for copy in loads(b):
            copy.start()
        return carry

    def select(b, carry):
        for k in range(KS):
            bsel_ref[k, b] = bias_ref[ids[k, b]]
            live_ref[k, b] = jnp.full((1, LB), (k < counts[b]).astype(F32), F32)
        return carry

    def work(b, carry):
        for copy in loads(b):
            copy.wait()
        pre = dot(cap_v[rows_of(b, TB)], tiles_v[b], 1, 0).astype(BF16)
        for k in range(KS):
            pre_ref[b, pl.ds(k * TB, TB)] = pre[:, k * LB:(k + 1) * LB]
        return carry

    lax.fori_loop(0, blocks, begin, 0)
    lax.fori_loop(0, blocks, select, 0)
    lax.fori_loop(0, blocks, work, 0)


def partial_pre(ids, counts, captured, enc_weight, enc_bias):
    tokens, features = captured.shape
    blocks = tokens // TB
    whole = pl.BlockSpec(memory_space=VMEM)
    outside = pl.BlockSpec(memory_space=pltpu.HBM)
    scalars = pl.BlockSpec(memory_space=pltpu.SMEM)
    return pl.pallas_call(
        pre_kernel,
        in_specs=[scalars, scalars, outside, outside, whole],
        out_specs=[whole] * 3,
        scratch_shapes=[
            VMEM((tokens, features), BF16), VMEM((blocks, features, KS * LB), BF16),
            pltpu.SemaphoreType.DMA((blocks,)), pltpu.SemaphoreType.DMA((blocks * KS,)),
        ],
        out_shape=[
            jax.ShapeDtypeStruct((blocks, KS * TB, LB), BF16),
            jax.ShapeDtypeStruct((KS, blocks, 1, LB), F32),
            jax.ShapeDtypeStruct((KS, blocks, 1, LB), F32),
        ],
        compiler_params=pltpu.CompilerParams(vmem_limit_bytes=BIG),
        name="partial_pre",
    )(ids, counts, captured, enc_weight, enc_bias.reshape(-1, 1, LB))


def spans(cuts):
    return [(lo, hi) for lo, hi in zip(cuts[:-1], cuts[1:]) if lo < hi]


def middle_kernel(
    n, nz, chunk, lag, first_spans, last_spans,
    ids, pre_ref, bias_ref, live_ref, dbias_ref, cap_hbm, dec_hbm,
    codes_ref, dpre_ref, delta_hbm, capt_hbm,
    cap_v, dec_v, part_v, delta_v, capt_v, up_in, down_in, up_out, down_out,
    pre_in, dc_out, dc_in,
    up_send, up_recv, down_send, down_recv,
    pre_send, pre_recv, code_send, code_recv, dc_send, dc_recv, dp_send, dp_recv,
    load_sem, store_sem, capt_sem,
):
    me = lax.axis_index("tok")
    z = lax.axis_index("lat")
    blocks, rows = pre_ref.shape[0], pre_ref.shape[1]
    share = rows // n
    slot = me * share // TB
    per = TB // chunk
    chunks = blocks * per
    has_low = z > 0
    has_high = z < nz - 1
    inner = jnp.logical_and(has_low, has_high)
    low = jnp.maximum(z - 1, 0)
    high = jnp.minimum(z + 1, nz - 1)

    load_dec = pltpu.make_async_copy(dec_hbm, dec_v, load_sem.at[0])
    load_cap = pltpu.make_async_copy(cap_hbm, cap_v, load_sem.at[1])
    load_dec.start()
    load_cap.start()

    barrier = pltpu.get_barrier_semaphore()
    for d in range(1, n):
        pl.semaphore_signal(barrier, inc=1, device_id={"tok": lax.rem(me + d, n)}, device_id_type=MESH)

    @pl.when(has_low)
    def _():
        pl.semaphore_signal(barrier, inc=1, device_id={"lat": low}, device_id_type=MESH)

    @pl.when(has_high)
    def _():
        pl.semaphore_signal(barrier, inc=1, device_id={"lat": high}, device_id_type=MESH)

    pl.semaphore_wait(barrier, n - 1 + has_low.astype(jnp.int32) + has_high.astype(jnp.int32))

    def share_of(j):
        return rows_of(j, share)

    def scatter(src, dst, send, recv, all_spans, i, d):
        lo, hi = all_spans[i]
        peer = lax.rem(me + d, n)
        at = i * (n - 1) + d - 1
        return pltpu.make_async_remote_copy(
            src_ref=src.at[lo:hi, share_of(peer)], dst_ref=dst.at[d - 1, lo:hi],
            send_sem=send.at[at], recv_sem=recv.at[at], device_id={"tok": peer}, device_id_type=MESH,
        )

    def gather(buf, send, recv, all_spans, i, d, owner):
        lo, hi = all_spans[i]
        at = i * (n - 1) + d - 1
        part = buf.at[lo:hi, share_of(owner)]
        return pltpu.make_async_remote_copy(
            src_ref=part, dst_ref=part, send_sem=send.at[at], recv_sem=recv.at[at],
            device_id={"tok": lax.rem(me + n - d, n)}, device_id_type=MESH,
        )

    def pre_copy(i, d):
        return scatter(pre_ref, pre_in, pre_send, pre_recv, first_spans, i, d)

    def dc_copy(i, d):
        return scatter(dc_out, dc_in, dc_send, dc_recv, last_spans, i, d)

    def code_copy(i, d, owner):
        return gather(codes_ref, code_send, code_recv, first_spans, i, d, owner)

    def dp_copy(i, d, owner):
        return gather(dpre_ref, dp_send, dp_recv, last_spans, i, d, owner)

    def other(d):
        return lax.rem(me + d, n)

    def activate(i):
        lo, hi = first_spans[i]
        total = pre_ref[lo:hi, share_of(me)].astype(F32)
        for d in range(1, n):
            pre_copy(i, d).wait_recv()
            total = total + pre_in[d - 1, lo:hi].astype(F32)
        v = total + bias_ref[slot, lo:hi]
        soft = jnp.maximum(v, 0.0) + jnp.log1p(jnp.exp(-jnp.abs(v)))
        codes_ref[lo:hi, share_of(me)] = (soft * live_ref[slot, lo:hi]).astype(BF16)
        for d in range(1, n):
            code_copy(i, d, me).start()

    def codes_here(i):
        for d in range(1, n):
            code_copy(i, d, other(d)).wait_recv()

    def slopes(i):
        lo, hi = last_spans[i]
        total = dc_out[lo:hi, share_of(me)].astype(F32)
        for d in range(1, n):
            dc_copy(i, d).wait_recv()
            total = total + dc_in[d - 1, lo:hi].astype(F32)
        rate = 1.0 - jnp.exp(-codes_ref[lo:hi, share_of(me)].astype(F32))
        dpre_ref[lo:hi, share_of(me)] = ((total + PENALTY) * rate).astype(BF16)
        for d in range(1, n):
            dp_copy(i, d, me).start()

    for i in range(len(first_spans)):
        for d in range(1, n):
            pre_copy(i, d).start()
    activate(0)
    load_dec.wait()
    codes_here(0)

    def chunk_rows(c):
        return rows_of(c, chunk)

    def line_copy(src, dst, send, recv, c, dev):
        return pltpu.make_async_remote_copy(
            src_ref=src.at[chunk_rows(c)], dst_ref=dst.at[chunk_rows(c)], send_sem=send.at[c], recv_sem=recv.at[c],
            device_id={"lat": dev}, device_id_type=MESH,
        )

    def up(c):
        return line_copy(up_out, up_in, up_send, up_recv, c, high)

    def up_first(c):
        return line_copy(part_v, up_in, up_send, up_recv, c, high)

    def down(c):
        return line_copy(down_out, down_in, down_send, down_recv, c, low)

    def down_first(c):
        return line_copy(part_v, down_in, down_send, down_recv, c, low)

    def dec_tile(b):
        return jnp.concatenate([dec_v[ids[k, b]] for k in range(KS)], axis=0)

    def make_part(b):
        tiles = [codes_ref[b, pl.ds(k * TB, TB)] for k in range(KS)]
        part_v[rows_of(b, TB)] = dot(jnp.concatenate(tiles, axis=1), dec_tile(b), 1, 0).astype(BF16)

    def delta_copy(b):
        return pltpu.make_async_copy(delta_v.at[rows_of(b, TB)], delta_hbm.at[rows_of(b, TB)], store_sem.at[b])

    def capt_copy(b):
        return pltpu.make_async_copy(capt_v.at[b], capt_hbm.at[b], capt_sem.at[b])

    up_delay = lag * z
    down_delay = lag * (nz - 1 - z)
    first_delay = jnp.minimum(up_delay, down_delay)
    last_delay = jnp.maximum(up_delay, down_delay)

    def step(t, carry):
        cf = t - first_delay
        cu = t - up_delay
        cd = t - down_delay
        cl = t - last_delay
        stage = jnp.maximum(cf, 0) // per
        fresh = jnp.logical_and(cf >= 0, cf < chunks)

        @pl.when(jnp.logical_and(fresh, lax.rem(jnp.maximum(cf, 0), per) == 0))
        def _():
            for i in range(1, len(first_spans)):
                @pl.when(stage == first_spans[i][0])
                def _():
                    codes_here(i)

            make_part(stage)

        for i in range(1, len(first_spans)):
            @pl.when(cf == first_spans[i - 1][1] * per - per // 2 - 1)
            def _():
                activate(i)

        @pl.when(jnp.logical_and(cu >= 0, cu < chunks))
        def _():
            @pl.when(has_low)
            def _():
                up(cu).wait_recv()

                @pl.when(has_high)
                def _():
                    up_out[chunk_rows(cu)] = (
                        up_in[chunk_rows(cu)].astype(F32) + part_v[chunk_rows(cu)].astype(F32)
                    ).astype(BF16)
                    up(cu).start()

            @pl.when(jnp.logical_not(has_low))
            def _():
                up_first(cu).start()

        @pl.when(jnp.logical_and(cd >= 0, cd < chunks))
        def _():
            @pl.when(has_high)
            def _():
                down(cd).wait_recv()

                @pl.when(has_low)
                def _():
                    down_out[chunk_rows(cd)] = (
                        down_in[chunk_rows(cd)].astype(F32) + part_v[chunk_rows(cd)].astype(F32)
                    ).astype(BF16)
                    down(cd).start()

            @pl.when(jnp.logical_not(has_high))
            def _():
                down_first(cd).start()

        @pl.when(cf == 0)
        def _():
            load_cap.wait()

        @pl.when(jnp.logical_and(fresh, lax.rem(jnp.maximum(cf, 0), per) == per // 2))
        def _():
            capt_v[stage] = cap_v[rows_of(stage, TB)].T
            capt_copy(stage).start()

        @pl.when(jnp.logical_and(cl >= 0, cl < chunks))
        def _():
            at = chunk_rows(cl)
            here = part_v[at].astype(F32) + dbias_ref[...] - cap_v[at].astype(F32)

            @pl.when(inner)
            def _():
                both = up_in[at].astype(F32) + down_in[at].astype(F32)
                delta_v[at] = (SCALE_ERR * (here + both)).astype(BF16)

            @pl.when(jnp.logical_not(has_low))
            def _():
                delta_v[at] = (SCALE_ERR * (here + down_in[at].astype(F32))).astype(BF16)

            @pl.when(jnp.logical_not(has_high))
            def _():
                delta_v[at] = (SCALE_ERR * (here + up_in[at].astype(F32))).astype(BF16)

            done = cl // per

            @pl.when(lax.rem(cl, per) == per - 1)
            def _():
                value = dot(delta_v[rows_of(done, TB)], dec_tile(done), 1, 1).astype(BF16)
                for k in range(KS):
                    dc_out[done, pl.ds(k * TB, TB)] = value[:, k * LB:(k + 1) * LB]
                delta_copy(done).start()

                for i in range(len(last_spans)):
                    @pl.when(done == last_spans[i][1] - 1)
                    def _():
                        for d in range(1, n):
                            dc_copy(i, d).start()

            for i in range(len(last_spans) - 1):
                @pl.when(cl == last_spans[i][1] * per - 1 + per // 2)
                def _():
                    slopes(i)

        return carry

    lax.fori_loop(0, chunks + lag * (nz - 1), step, 0)

    slopes(len(last_spans) - 1)

    def drain(c, carry):
        @pl.when(has_high)
        def _():
            up(c).wait_send()

        @pl.when(has_low)
        def _():
            down(c).wait_send()

        return carry

    lax.fori_loop(0, chunks, drain, 0)

    def stored(b, carry):
        delta_copy(b).wait()
        capt_copy(b).wait()
        return carry

    lax.fori_loop(0, blocks, stored, 0)
    for i in range(len(first_spans)):
        for d in range(1, n):
            pre_copy(i, d).wait_send()
            code_copy(i, d, me).wait_send()
    for i in range(len(last_spans)):
        for d in range(1, n):
            dc_copy(i, d).wait_send()
            dp_copy(i, d, me).wait_send()
            dp_copy(i, d, other(d)).wait_recv()


def middle(ids, pre, bias, live, dec_bias, captured, dec_weight, chunk, lag):
    n = lax.axis_size("tok")
    nz = lax.axis_size("lat")
    tokens, features = captured.shape
    blocks, rows, _ = pre.shape
    lat_dev = dec_weight.shape[0]
    chunks = tokens // chunk
    first_spans = spans([0, 1, blocks])
    last_spans = spans([0, max(blocks - 2, 0), max(blocks - 1, 0), blocks])
    whole = pl.BlockSpec(memory_space=VMEM)
    outside = pl.BlockSpec(memory_space=pltpu.HBM)
    sems = lambda count: [pltpu.SemaphoreType.DMA((count,))]
    wide = VMEM((tokens, features), BF16)
    shares = VMEM((n - 1, blocks, rows // n, LB), BF16)
    return pl.pallas_call(
        functools.partial(middle_kernel, n, nz, chunk, lag, first_spans, last_spans),
        out_shape=[
            jax.ShapeDtypeStruct((blocks, rows, LB), BF16),
            jax.ShapeDtypeStruct((blocks, rows, LB), BF16),
            jax.ShapeDtypeStruct((tokens, features), BF16),
            jax.ShapeDtypeStruct((blocks, features, TB), BF16),
        ],
        in_specs=[pl.BlockSpec(memory_space=pltpu.SMEM)] + [whole] * 4 + [outside] * 2,
        out_specs=[whole, whole, outside, outside],
        scratch_shapes=[wide, VMEM((lat_dev // LB, LB, features), BF16), wide, wide, VMEM((blocks, features, TB), BF16)]
        + [wide] * 4 + [shares, VMEM((blocks, rows, LB), BF16), shares]
        + sems(chunks) * 4 + sems((n - 1) * len(first_spans)) * 4 + sems((n - 1) * len(last_spans)) * 4
        + sems(2) + sems(blocks) * 2,
        compiler_params=pltpu.CompilerParams(
            collective_id=0, has_side_effects=True, vmem_limit_bytes=BIG
        ),
        name="middle",
    )(
        ids, pre, bias, live, dec_bias.reshape(1, features), captured,
        dec_weight.reshape(-1, LB, features),
    )


def grads_kernel(
    ids, delta_hbm, capt_hbm, codes_ref, dpre_ref,
    enc_hbm, dec_hbm, delta_v, capt_v, zero_e, zero_d, out_e, out_d, acc_e, acc_d,
    members, seen, place, spare, delta_sem, capt_sem, enc_sem, dec_sem,
):
    blocks = capt_v.shape[0]
    groups = members.shape[0]

    def loads(b):
        return (
            pltpu.make_async_copy(delta_hbm.at[rows_of(b, TB)], delta_v.at[rows_of(b, TB)], delta_sem.at[b]),
            pltpu.make_async_copy(capt_hbm.at[b], capt_v.at[b], capt_sem.at[b]),
        )

    def enc_copy(src, g):
        return pltpu.make_async_copy(src, enc_hbm.at[:, rows_of(g, LB)], enc_sem.at[g])

    def dec_copy(src, g):
        return pltpu.make_async_copy(src, dec_hbm.at[rows_of(g, LB)], dec_sem.at[g])

    def begin(b, carry):
        for copy in loads(b):
            copy.start()
        return carry

    def clear(g, carry):
        members[g] = 0
        seen[g] = 0
        return carry

    def count(b, carry):
        for k in range(KS):
            members[ids[k, b]] += 1
        return carry

    def blank(g, carry):
        @pl.when(members[g] == 0)
        def _():
            enc_copy(zero_e, g).start()
            dec_copy(zero_d, g).start()

        return carry

    lax.fori_loop(0, blocks, begin, 0)
    zero_e[...] = jnp.zeros(zero_e.shape, BF16)
    zero_d[...] = jnp.zeros(zero_d.shape, BF16)
    lax.fori_loop(0, groups, clear, 0)
    lax.fori_loop(0, blocks, count, 0)
    lax.fori_loop(0, groups, blank, 0)
    spare[0] = 0

    def work(b, carry):
        for copy in loads(b):
            copy.wait()
        for k in range(KS):
            g = ids[k, b]
            s = b * KS + k
            total = members[g]
            before = seen[g]
            seen[g] = before + 1

            def enc_tile():
                return dot(capt_v[b], dpre_ref[b, pl.ds(k * TB, TB)], 1, 0)

            def dec_tile():
                return dot(codes_ref[b, pl.ds(k * TB, TB)], delta_v[rows_of(b, TB)], 0, 0)

            @pl.when(total == 1)
            def _():
                out_e[s] = enc_tile().astype(BF16)
                out_d[s] = dec_tile().astype(BF16)

            @pl.when(total > 1)
            def _():
                @pl.when(before == 0)
                def _():
                    at = spare[0]
                    spare[0] = at + 1
                    place[g] = at
                    acc_e[at] = enc_tile()
                    acc_d[at] = dec_tile()

                @pl.when(before > 0)
                def _():
                    at = place[g]
                    e = acc_e[at] + enc_tile()
                    d = acc_d[at] + dec_tile()

                    @pl.when(before + 1 < total)
                    def _():
                        acc_e[at] = e
                        acc_d[at] = d

                    @pl.when(before + 1 == total)
                    def _():
                        out_e[s] = e.astype(BF16)
                        out_d[s] = d.astype(BF16)

            @pl.when(before + 1 == total)
            def _():
                enc_copy(out_e.at[s], g).start()
                dec_copy(out_d.at[s], g).start()

        return carry

    lax.fori_loop(0, blocks, work, 0)

    def finish(g, carry):
        enc_copy(zero_e, g).wait()
        dec_copy(zero_d, g).wait()
        return carry

    lax.fori_loop(0, groups, finish, 0)


def gradients(ids, delta, capt, codes, dpre, groups):
    tokens, features = delta.shape
    blocks = tokens // TB
    slots = blocks * KS
    whole = pl.BlockSpec(memory_space=VMEM)
    outside = pl.BlockSpec(memory_space=pltpu.HBM)
    shared = max(min(slots // 2, groups), 1)
    return pl.pallas_call(
        grads_kernel,
        in_specs=[pl.BlockSpec(memory_space=pltpu.SMEM), outside, outside, whole, whole],
        out_specs=[outside, outside],
        scratch_shapes=[
            VMEM((tokens, features), BF16), VMEM((blocks, features, TB), BF16),
            VMEM((features, LB), BF16), VMEM((LB, features), BF16),
            VMEM((slots, features, LB), BF16), VMEM((slots, LB, features), BF16),
            VMEM((shared, features, LB), F32), VMEM((shared, LB, features), F32),
            pltpu.SMEM((groups,), jnp.int32), pltpu.SMEM((groups,), jnp.int32),
            pltpu.SMEM((groups,), jnp.int32), pltpu.SMEM((1,), jnp.int32),
            pltpu.SemaphoreType.DMA((blocks,)), pltpu.SemaphoreType.DMA((blocks,)),
            pltpu.SemaphoreType.DMA((groups,)), pltpu.SemaphoreType.DMA((groups,)),
        ],
        out_shape=[
            jax.ShapeDtypeStruct((features, groups * LB), BF16),
            jax.ShapeDtypeStruct((groups * LB, features), BF16),
        ],
        compiler_params=pltpu.CompilerParams(vmem_limit_bytes=BIG),
        name="gradients",
    )(ids, delta, capt, codes, dpre)


def local(captured, enc_weight, enc_bias, dec_weight, dec_bias, block_ids, block_counts):
    ids = block_ids.transpose(1, 2, 0).reshape(KS, -1)
    counts = block_counts.reshape(-1)
    pre, bias, live = partial_pre(ids, counts, captured, enc_weight, enc_bias)
    codes, dpre, delta, capt = middle(ids, pre, bias, live, dec_bias, captured, dec_weight, CHUNK, LAG)
    return tuple(gradients(ids, delta, capt, codes, dpre, dec_weight.shape[0] // LB))


def solution(mesh):
    in_specs = (
        P(None, "tok"),
        P("tok", "lat"),
        P("lat"),
        P("lat", "tok"),
        P("tok"),
        P(None, "lat", None),
        P(None, "lat"),
    )
    out_specs = (P("tok", "lat"), P("lat", "tok"))
    return jax.shard_map(local, mesh=mesh, in_specs=in_specs, out_specs=out_specs, check_vma=False)
```

```python
import functools

import jax
import jax.numpy as jnp
from jax import lax
from jax.experimental import pallas as pl
from jax.experimental.pallas import tpu as pltpu
from jax.sharding import PartitionSpec as P

TB = 128
LB = 128
KS = 2

SCALE_ERR = 0.0625
PENALTY = 0.05
CHUNK = 16
LAG = 3
F32 = jnp.float32
BF16 = jnp.bfloat16
MESH = pl.DeviceIdType.MESH
VMEM = pltpu.VMEM
BIG = 52 * 1024 * 1024
MIDDLE = 43 * 1024 * 1024
LAST = 36 * 1024 * 1024


def dot(a, b, ca, cb):
    return lax.dot_general(a, b, (((ca,), (cb,)), ((), ())), preferred_element_type=F32)


def rows_of(b, size):
    return pl.ds(pl.multiple_of(b * size, size), size)


def pre_kernel(ids, counts, cap_hbm, enc_hbm, bias_ref, pre_ref, bsel_ref, live_ref, cap_v, tiles_v, cap_sem, tile_sem):
    blocks = pre_ref.shape[0]

    def loads(b):
        copies = [pltpu.make_async_copy(cap_hbm.at[rows_of(b, TB)], cap_v.at[rows_of(b, TB)], cap_sem.at[b])]
        for k in range(KS):
            copies.append(pltpu.make_async_copy(
                enc_hbm.at[:, rows_of(ids[k, b], LB)], tiles_v.at[b, :, pl.ds(k * LB, LB)], tile_sem.at[b * KS + k]
            ))
        return copies

    def begin(b, carry):
        for copy in loads(b):
            copy.start()
        return carry

    def select(b, carry):
        for k in range(KS):
            bsel_ref[k, b] = bias_ref[ids[k, b]]
            live_ref[k, b] = jnp.full((1, LB), (k < counts[b]).astype(F32), F32)
        return carry

    def work(b, carry):
        for copy in loads(b):
            copy.wait()
        pre = dot(cap_v[rows_of(b, TB)], tiles_v[b], 1, 0).astype(BF16)
        for k in range(KS):
            pre_ref[b, pl.ds(k * TB, TB)] = pre[:, k * LB:(k + 1) * LB]
        return carry

    lax.fori_loop(0, blocks, begin, 0)
    lax.fori_loop(0, blocks, select, 0)
    lax.fori_loop(0, blocks, work, 0)


def partial_pre(ids, counts, captured, enc_weight, enc_bias):
    tokens, features = captured.shape
    blocks = tokens // TB
    whole = pl.BlockSpec(memory_space=VMEM)
    outside = pl.BlockSpec(memory_space=pltpu.HBM)
    scalars = pl.BlockSpec(memory_space=pltpu.SMEM)
    return pl.pallas_call(
        pre_kernel,
        in_specs=[scalars, scalars, outside, outside, whole],
        out_specs=[whole] * 3,
        scratch_shapes=[
            VMEM((tokens, features), BF16), VMEM((blocks, features, KS * LB), BF16),
            pltpu.SemaphoreType.DMA((blocks,)), pltpu.SemaphoreType.DMA((blocks * KS,)),
        ],
        out_shape=[
            jax.ShapeDtypeStruct((blocks, KS * TB, LB), BF16),
            jax.ShapeDtypeStruct((KS, blocks, 1, LB), F32),
            jax.ShapeDtypeStruct((KS, blocks, 1, LB), F32),
        ],
        compiler_params=pltpu.CompilerParams(vmem_limit_bytes=BIG),
        name="partial_pre",
    )(ids, counts, captured, enc_weight, enc_bias.reshape(-1, 1, LB))


def spans(cuts):
    return [(lo, hi) for lo, hi in zip(cuts[:-1], cuts[1:]) if lo < hi]


def middle_kernel(
    n, nz, chunk, lag, first_spans, last_spans,
    ids, pre_ref, bias_ref, live_ref, dbias_ref, cap_hbm, dec_hbm,
    codes_ref, dpre_ref, delta_v, capt_v,
    cap_v, dec_v, part_v, up_in, down_in, up_out, down_out,
    pre_in, dc_out, dc_in,
    up_send, up_recv, down_send, down_recv,
    pre_send, pre_recv, code_send, code_recv, dc_send, dc_recv, dp_send, dp_recv,
    load_sem,
):
    me = lax.axis_index("tok")
    z = lax.axis_index("lat")
    blocks, rows = pre_ref.shape[0], pre_ref.shape[1]
    share = rows // n
    slot = me * share // TB
    per = TB // chunk
    chunks = blocks * per
    has_low = z > 0
    has_high = z < nz - 1
    inner = jnp.logical_and(has_low, has_high)
    low = jnp.maximum(z - 1, 0)
    high = jnp.minimum(z + 1, nz - 1)

    load_dec = pltpu.make_async_copy(dec_hbm, dec_v, load_sem.at[0])
    load_cap = pltpu.make_async_copy(cap_hbm, cap_v, load_sem.at[1])
    load_dec.start()

    barrier = pltpu.get_barrier_semaphore()
    for d in range(1, n):
        pl.semaphore_signal(barrier, inc=1, device_id={"tok": lax.rem(me + d, n)}, device_id_type=MESH)

    @pl.when(has_low)
    def _():
        pl.semaphore_signal(barrier, inc=1, device_id={"lat": low}, device_id_type=MESH)

    @pl.when(has_high)
    def _():
        pl.semaphore_signal(barrier, inc=1, device_id={"lat": high}, device_id_type=MESH)

    pl.semaphore_wait(barrier, n - 1 + has_low.astype(jnp.int32) + has_high.astype(jnp.int32))

    def share_of(j):
        return rows_of(j, share)

    def scatter(src, dst, send, recv, all_spans, i, d):
        lo, hi = all_spans[i]
        peer = lax.rem(me + d, n)
        at = i * (n - 1) + d - 1
        return pltpu.make_async_remote_copy(
            src_ref=src.at[lo:hi, share_of(peer)], dst_ref=dst.at[d - 1, lo:hi],
            send_sem=send.at[at], recv_sem=recv.at[at], device_id={"tok": peer}, device_id_type=MESH,
        )

    def gather(buf, send, recv, all_spans, i, d, owner):
        lo, hi = all_spans[i]
        at = i * (n - 1) + d - 1
        part = buf.at[lo:hi, share_of(owner)]
        return pltpu.make_async_remote_copy(
            src_ref=part, dst_ref=part, send_sem=send.at[at], recv_sem=recv.at[at],
            device_id={"tok": lax.rem(me + n - d, n)}, device_id_type=MESH,
        )

    def pre_copy(i, d):
        return scatter(pre_ref, pre_in, pre_send, pre_recv, first_spans, i, d)

    def dc_copy(i, d):
        return scatter(dc_out, dc_in, dc_send, dc_recv, last_spans, i, d)

    def code_copy(i, d, owner):
        return gather(codes_ref, code_send, code_recv, first_spans, i, d, owner)

    def dp_copy(i, d, owner):
        return gather(dpre_ref, dp_send, dp_recv, last_spans, i, d, owner)

    def other(d):
        return lax.rem(me + d, n)

    def activate(i):
        lo, hi = first_spans[i]
        total = pre_ref[lo:hi, share_of(me)].astype(F32)
        for d in range(1, n):
            pre_copy(i, d).wait_recv()
            total = total + pre_in[d - 1, lo:hi].astype(F32)
        v = total + bias_ref[slot, lo:hi]
        soft = jnp.maximum(v, 0.0) + jnp.log1p(jnp.exp(-jnp.abs(v)))
        codes_ref[lo:hi, share_of(me)] = (soft * live_ref[slot, lo:hi]).astype(BF16)
        for d in range(1, n):
            code_copy(i, d, me).start()

    def codes_here(i):
        for d in range(1, n):
            code_copy(i, d, other(d)).wait_recv()

    def slopes(i):
        lo, hi = last_spans[i]
        total = dc_out[lo:hi, share_of(me)].astype(F32)
        for d in range(1, n):
            dc_copy(i, d).wait_recv()
            total = total + dc_in[d - 1, lo:hi].astype(F32)
        rate = 1.0 - jnp.exp(-codes_ref[lo:hi, share_of(me)].astype(F32))
        dpre_ref[lo:hi, share_of(me)] = ((total + PENALTY) * rate).astype(BF16)
        for d in range(1, n):
            dp_copy(i, d, me).start()

    for d in range(1, n):
        pre_copy(0, d).start()
    activate(0)
    for i in range(1, len(first_spans)):
        for d in range(1, n):
            pre_copy(i, d).start()
    load_dec.wait()
    load_cap.start()
    codes_here(0)

    def chunk_rows(c):
        return rows_of(c, chunk)

    def line_copy(src, dst, send, recv, c, dev):
        return pltpu.make_async_remote_copy(
            src_ref=src.at[chunk_rows(c)], dst_ref=dst.at[chunk_rows(c)], send_sem=send.at[c], recv_sem=recv.at[c],
            device_id={"lat": dev}, device_id_type=MESH,
        )

    def up(c):
        return line_copy(up_out, up_in, up_send, up_recv, c, high)

    def up_first(c):
        return line_copy(part_v, up_in, up_send, up_recv, c, high)

    def down(c):
        return line_copy(down_out, down_in, down_send, down_recv, c, low)

    def down_first(c):
        return line_copy(part_v, down_in, down_send, down_recv, c, low)

    def dec_tile(b):
        return jnp.concatenate([dec_v[ids[k, b]] for k in range(KS)], axis=0)

    def make_part(b):
        tiles = [codes_ref[b, pl.ds(k * TB, TB)] for k in range(KS)]
        part_v[rows_of(b, TB)] = dot(jnp.concatenate(tiles, axis=1), dec_tile(b), 1, 0).astype(BF16)

    up_delay = lag * z
    down_delay = lag * (nz - 1 - z)
    first_delay = jnp.minimum(up_delay, down_delay)
    last_delay = jnp.maximum(up_delay, down_delay)

    def step(t, carry):
        cf = t - first_delay
        cu = t - up_delay
        cd = t - down_delay
        cl = t - last_delay
        stage = jnp.maximum(cf, 0) // per
        fresh = jnp.logical_and(cf >= 0, cf < chunks)

        @pl.when(jnp.logical_and(fresh, lax.rem(jnp.maximum(cf, 0), per) == 0))
        def _():
            for i in range(1, len(first_spans)):
                @pl.when(stage == first_spans[i][0])
                def _():
                    codes_here(i)

            make_part(stage)

        for i in range(1, len(first_spans)):
            @pl.when(cf == first_spans[i - 1][1] * per - per // 2 - 1)
            def _():
                activate(i)

        @pl.when(jnp.logical_and(cu >= 0, cu < chunks))
        def _():
            @pl.when(has_low)
            def _():
                up(cu).wait_recv()

                @pl.when(has_high)
                def _():
                    up_out[chunk_rows(cu)] = (
                        up_in[chunk_rows(cu)].astype(F32) + part_v[chunk_rows(cu)].astype(F32)
                    ).astype(BF16)
                    up(cu).start()

            @pl.when(jnp.logical_not(has_low))
            def _():
                up_first(cu).start()

        @pl.when(jnp.logical_and(cd >= 0, cd < chunks))
        def _():
            @pl.when(has_high)
            def _():
                down(cd).wait_recv()

                @pl.when(has_low)
                def _():
                    down_out[chunk_rows(cd)] = (
                        down_in[chunk_rows(cd)].astype(F32) + part_v[chunk_rows(cd)].astype(F32)
                    ).astype(BF16)
                    down(cd).start()

            @pl.when(jnp.logical_not(has_high))
            def _():
                down_first(cd).start()

        @pl.when(cf == 0)
        def _():
            load_cap.wait()

        @pl.when(jnp.logical_and(fresh, lax.rem(jnp.maximum(cf, 0), per) == per // 2))
        def _():
            capt_v[stage] = cap_v[rows_of(stage, TB)].T

        @pl.when(jnp.logical_and(cl >= 0, cl < chunks))
        def _():
            at = chunk_rows(cl)
            here = part_v[at].astype(F32) + dbias_ref[...] - cap_v[at].astype(F32)

            @pl.when(inner)
            def _():
                both = up_in[at].astype(F32) + down_in[at].astype(F32)
                delta_v[at] = (SCALE_ERR * (here + both)).astype(BF16)

            @pl.when(jnp.logical_not(has_low))
            def _():
                delta_v[at] = (SCALE_ERR * (here + down_in[at].astype(F32))).astype(BF16)

            @pl.when(jnp.logical_not(has_high))
            def _():
                delta_v[at] = (SCALE_ERR * (here + up_in[at].astype(F32))).astype(BF16)

            done = cl // per

            @pl.when(lax.rem(cl, per) == per - 1)
            def _():
                value = dot(delta_v[rows_of(done, TB)], dec_tile(done), 1, 1).astype(BF16)
                for k in range(KS):
                    dc_out[done, pl.ds(k * TB, TB)] = value[:, k * LB:(k + 1) * LB]

                for i in range(len(last_spans)):
                    @pl.when(done == last_spans[i][1] - 1)
                    def _():
                        for d in range(1, n):
                            dc_copy(i, d).start()

            for i in range(len(last_spans) - 1):
                @pl.when(cl == last_spans[i][1] * per - 1 + per // 2)
                def _():
                    slopes(i)

        return carry

    lax.fori_loop(0, chunks + lag * (nz - 1), step, 0)

    slopes(len(last_spans) - 1)

    def drain(c, carry):
        @pl.when(has_high)
        def _():
            up(c).wait_send()

        @pl.when(has_low)
        def _():
            down(c).wait_send()

        return carry

    lax.fori_loop(0, chunks, drain, 0)

    for i in range(len(first_spans)):
        for d in range(1, n):
            pre_copy(i, d).wait_send()
            code_copy(i, d, me).wait_send()
    for i in range(len(last_spans)):
        for d in range(1, n):
            dc_copy(i, d).wait_send()
            dp_copy(i, d, me).wait_send()
            dp_copy(i, d, other(d)).wait_recv()


def middle(ids, pre, bias, live, dec_bias, captured, dec_weight, chunk, lag):
    n = lax.axis_size("tok")
    nz = lax.axis_size("lat")
    tokens, features = captured.shape
    blocks, rows, _ = pre.shape
    lat_dev = dec_weight.shape[0]
    chunks = tokens // chunk
    first_spans = spans([0, 1, blocks])
    last_spans = spans([0, max(blocks - 2, 0), max(blocks - 1, 0), blocks])
    whole = pl.BlockSpec(memory_space=VMEM)
    outside = pl.BlockSpec(memory_space=pltpu.HBM)
    sems = lambda count: [pltpu.SemaphoreType.DMA((count,))]
    wide = VMEM((tokens, features), BF16)
    shares = VMEM((n - 1, blocks, rows // n, LB), BF16)
    return pl.pallas_call(
        functools.partial(middle_kernel, n, nz, chunk, lag, first_spans, last_spans),
        out_shape=[
            jax.ShapeDtypeStruct((blocks, rows, LB), BF16),
            jax.ShapeDtypeStruct((blocks, rows, LB), BF16),
            jax.ShapeDtypeStruct((tokens, features), BF16),
            jax.ShapeDtypeStruct((blocks, features, TB), BF16),
        ],
        in_specs=[pl.BlockSpec(memory_space=pltpu.SMEM)] + [whole] * 4 + [outside] * 2,
        out_specs=[whole] * 4,
        scratch_shapes=[wide, VMEM((lat_dev // LB, LB, features), BF16), wide]
        + [wide] * 4 + [shares, VMEM((blocks, rows, LB), BF16), shares]
        + sems(chunks) * 4 + sems((n - 1) * len(first_spans)) * 4 + sems((n - 1) * len(last_spans)) * 4
        + sems(2),
        compiler_params=pltpu.CompilerParams(
            collective_id=0, has_side_effects=True, vmem_limit_bytes=MIDDLE
        ),
        name="middle",
    )(
        ids, pre, bias, live, dec_bias.reshape(1, features), captured,
        dec_weight.reshape(-1, LB, features),
    )


def grads_kernel(
    ids, delta_v, capt_v, codes_ref, dpre_ref,
    enc_hbm, dec_hbm, zero_e, zero_d, out_e, out_d, acc_e, acc_d,
    members, seen, place, spare, enc_sem, dec_sem,
):
    blocks = capt_v.shape[0]
    groups = members.shape[0]

    def enc_copy(src, g):
        return pltpu.make_async_copy(src, enc_hbm.at[:, rows_of(g, LB)], enc_sem.at[g])

    def dec_copy(src, g):
        return pltpu.make_async_copy(src, dec_hbm.at[rows_of(g, LB)], dec_sem.at[g])

    def clear(g, carry):
        members[g] = 0
        seen[g] = 0
        return carry

    def count(b, carry):
        for k in range(KS):
            members[ids[k, b]] += 1
        return carry

    def blank(g, carry):
        @pl.when(members[g] == 0)
        def _():
            enc_copy(zero_e, g).start()
            dec_copy(zero_d, g).start()

        return carry

    zero_e[...] = jnp.zeros(zero_e.shape, BF16)
    zero_d[...] = jnp.zeros(zero_d.shape, BF16)
    lax.fori_loop(0, groups, clear, 0)
    lax.fori_loop(0, blocks, count, 0)
    lax.fori_loop(0, groups, blank, 0)
    spare[0] = 0

    def work(b, carry):
        for k in range(KS):
            g = ids[k, b]
            s = b * KS + k
            total = members[g]
            before = seen[g]
            seen[g] = before + 1

            def enc_tile():
                return dot(capt_v[b], dpre_ref[b, pl.ds(k * TB, TB)], 1, 0)

            def dec_tile():
                return dot(codes_ref[b, pl.ds(k * TB, TB)], delta_v[rows_of(b, TB)], 0, 0)

            @pl.when(total == 1)
            def _():
                out_e[s] = enc_tile().astype(BF16)
                out_d[s] = dec_tile().astype(BF16)

            @pl.when(total > 1)
            def _():
                @pl.when(before == 0)
                def _():
                    at = spare[0]
                    spare[0] = at + 1
                    place[g] = at
                    acc_e[at] = enc_tile()
                    acc_d[at] = dec_tile()

                @pl.when(before > 0)
                def _():
                    at = place[g]
                    e = acc_e[at] + enc_tile()
                    d = acc_d[at] + dec_tile()

                    @pl.when(before + 1 < total)
                    def _():
                        acc_e[at] = e
                        acc_d[at] = d

                    @pl.when(before + 1 == total)
                    def _():
                        out_e[s] = e.astype(BF16)
                        out_d[s] = d.astype(BF16)

            @pl.when(before + 1 == total)
            def _():
                enc_copy(out_e.at[s], g).start()
                dec_copy(out_d.at[s], g).start()

        return carry

    lax.fori_loop(0, blocks, work, 0)

    def finish(g, carry):
        enc_copy(zero_e, g).wait()
        dec_copy(zero_d, g).wait()
        return carry

    lax.fori_loop(0, groups, finish, 0)


def gradients(ids, delta, capt, codes, dpre, groups):
    tokens, features = delta.shape
    blocks = tokens // TB
    slots = blocks * KS
    whole = pl.BlockSpec(memory_space=VMEM)
    outside = pl.BlockSpec(memory_space=pltpu.HBM)
    shared = max(min(slots // 2, groups), 1)
    return pl.pallas_call(
        grads_kernel,
        in_specs=[pl.BlockSpec(memory_space=pltpu.SMEM)] + [whole] * 4,
        out_specs=[outside, outside],
        scratch_shapes=[
            VMEM((features, LB), BF16), VMEM((LB, features), BF16),
            VMEM((slots, features, LB), BF16), VMEM((slots, LB, features), BF16),
            VMEM((shared, features, LB), F32), VMEM((shared, LB, features), F32),
            pltpu.SMEM((groups,), jnp.int32), pltpu.SMEM((groups,), jnp.int32),
            pltpu.SMEM((groups,), jnp.int32), pltpu.SMEM((1,), jnp.int32),
            pltpu.SemaphoreType.DMA((groups,)), pltpu.SemaphoreType.DMA((groups,)),
        ],
        out_shape=[
            jax.ShapeDtypeStruct((features, groups * LB), BF16),
            jax.ShapeDtypeStruct((groups * LB, features), BF16),
        ],
        compiler_params=pltpu.CompilerParams(vmem_limit_bytes=LAST),
        name="gradients",
    )(ids, delta, capt, codes, dpre)


def local(captured, enc_weight, enc_bias, dec_weight, dec_bias, block_ids, block_counts):
    ids = block_ids.transpose(1, 2, 0).reshape(KS, -1)
    counts = block_counts.reshape(-1)
    pre, bias, live = partial_pre(ids, counts, captured, enc_weight, enc_bias)
    codes, dpre, delta, capt = middle(ids, pre, bias, live, dec_bias, captured, dec_weight, CHUNK, LAG)
    return tuple(gradients(ids, delta, capt, codes, dpre, dec_weight.shape[0] // LB))


def solution(mesh):
    in_specs = (
        P(None, "tok"),
        P("tok", "lat"),
        P("lat"),
        P("lat", "tok"),
        P("tok"),
        P(None, "lat", None),
        P(None, "lat"),
    )
    out_specs = (P("tok", "lat"), P("lat", "tok"))
    return jax.shard_map(local, mesh=mesh, in_specs=in_specs, out_specs=out_specs, check_vma=False)
```

```python
import functools

import jax
import jax.numpy as jnp
from jax import lax
from jax.experimental import pallas as pl
from jax.experimental.pallas import tpu as pltpu
from jax.sharding import PartitionSpec as P

TB = 128
LB = 128
KS = 2

SCALE_ERR = 0.0625
PENALTY = 0.05
CHUNK = 16
LAG = 3
F32 = jnp.float32
BF16 = jnp.bfloat16
MESH = pl.DeviceIdType.MESH
VMEM = pltpu.VMEM
BIG = 52 * 1024 * 1024
MIDDLE = 43 * 1024 * 1024
LAST = 36 * 1024 * 1024


def dot(a, b, ca, cb):
    return lax.dot_general(a, b, (((ca,), (cb,)), ((), ())), preferred_element_type=F32)


def rows_of(b, size):
    return pl.ds(pl.multiple_of(b * size, size), size)


def pre_kernel(
    ids, counts, cap_hbm, enc_hbm, bias_ref, pre_ref, bsel_ref, live_ref, egrad_hbm, dgrad_hbm,
    cap_v, tiles_v, zero_e, zero_d, members, cap_sem, tile_sem, enc_sem, dec_sem,
):
    blocks = pre_ref.shape[0]
    groups = members.shape[0]

    def clear(g, carry):
        members[g] = 0
        return carry

    def count(b, carry):
        for k in range(KS):
            members[ids[k, b]] += 1
        return carry

    def blanks(g):
        return (
            pltpu.make_async_copy(zero_e, egrad_hbm.at[:, rows_of(g, LB)], enc_sem.at[g]),
            pltpu.make_async_copy(zero_d, dgrad_hbm.at[rows_of(g, LB)], dec_sem.at[g]),
        )

    def blank(g, carry):
        @pl.when(members[g] == 0)
        def _():
            for copy in blanks(g):
                copy.start()

        return carry

    def blanked(g, carry):
        @pl.when(members[g] == 0)
        def _():
            for copy in blanks(g):
                copy.wait()

        return carry


    def loads(b):
        copies = [pltpu.make_async_copy(cap_hbm.at[rows_of(b, TB)], cap_v.at[rows_of(b, TB)], cap_sem.at[b])]
        for k in range(KS):
            copies.append(pltpu.make_async_copy(
                enc_hbm.at[:, rows_of(ids[k, b], LB)], tiles_v.at[b, :, pl.ds(k * LB, LB)], tile_sem.at[b * KS + k]
            ))
        return copies

    def begin(b, carry):
        for copy in loads(b):
            copy.start()
        return carry

    def select(b, carry):
        for k in range(KS):
            bsel_ref[k, b] = bias_ref[ids[k, b]]
            live_ref[k, b] = jnp.full((1, LB), (k < counts[b]).astype(F32), F32)
        return carry

    def work(b, carry):
        for copy in loads(b):
            copy.wait()
        pre = dot(cap_v[rows_of(b, TB)], tiles_v[b], 1, 0).astype(BF16)
        for k in range(KS):
            pre_ref[b, pl.ds(k * TB, TB)] = pre[:, k * LB:(k + 1) * LB]
        return carry

    lax.fori_loop(0, blocks, begin, 0)
    zero_e[...] = jnp.zeros(zero_e.shape, BF16)
    zero_d[...] = jnp.zeros(zero_d.shape, BF16)
    lax.fori_loop(0, groups, clear, 0)
    lax.fori_loop(0, blocks, count, 0)
    lax.fori_loop(0, groups, blank, 0)
    lax.fori_loop(0, blocks, select, 0)
    lax.fori_loop(0, blocks, work, 0)
    lax.fori_loop(0, groups, blanked, 0)


def partial_pre(ids, counts, captured, enc_weight, enc_bias):
    tokens, features = captured.shape
    blocks = tokens // TB
    groups = enc_weight.shape[1] // LB
    whole = pl.BlockSpec(memory_space=VMEM)
    outside = pl.BlockSpec(memory_space=pltpu.HBM)
    scalars = pl.BlockSpec(memory_space=pltpu.SMEM)
    return pl.pallas_call(
        pre_kernel,
        in_specs=[scalars, scalars, outside, outside, whole],
        out_specs=[whole] * 3 + [outside] * 2,
        scratch_shapes=[
            VMEM((tokens, features), BF16), VMEM((blocks, features, KS * LB), BF16),
            VMEM((features, LB), BF16), VMEM((LB, features), BF16), pltpu.SMEM((groups,), jnp.int32),
            pltpu.SemaphoreType.DMA((blocks,)), pltpu.SemaphoreType.DMA((blocks * KS,)),
            pltpu.SemaphoreType.DMA((groups,)), pltpu.SemaphoreType.DMA((groups,)),
        ],
        out_shape=[
            jax.ShapeDtypeStruct((blocks, KS * TB, LB), BF16),
            jax.ShapeDtypeStruct((KS, blocks, 1, LB), F32),
            jax.ShapeDtypeStruct((KS, blocks, 1, LB), F32),
            jax.ShapeDtypeStruct((features, groups * LB), BF16),
            jax.ShapeDtypeStruct((groups * LB, features), BF16),
        ],
        compiler_params=pltpu.CompilerParams(vmem_limit_bytes=BIG),
        name="partial_pre",
    )(ids, counts, captured, enc_weight, enc_bias.reshape(-1, 1, LB))


def spans(cuts):
    return [(lo, hi) for lo, hi in zip(cuts[:-1], cuts[1:]) if lo < hi]


def middle_kernel(
    n, nz, chunk, lag, first_spans, last_spans,
    ids, pre_ref, bias_ref, live_ref, dbias_ref, cap_hbm, dec_hbm,
    codes_ref, dpre_ref, delta_v, capt_v,
    cap_v, dec_v, part_v, up_in, down_in, up_out, down_out,
    pre_in, dc_out, dc_in,
    up_send, up_recv, down_send, down_recv,
    pre_send, pre_recv, code_send, code_recv, dc_send, dc_recv, dp_send, dp_recv,
    load_sem,
):
    me = lax.axis_index("tok")
    z = lax.axis_index("lat")
    blocks, rows = pre_ref.shape[0], pre_ref.shape[1]
    share = rows // n
    slot = me * share // TB
    per = TB // chunk
    chunks = blocks * per
    has_low = z > 0
    has_high = z < nz - 1
    inner = jnp.logical_and(has_low, has_high)
    low = jnp.maximum(z - 1, 0)
    high = jnp.minimum(z + 1, nz - 1)

    load_dec = pltpu.make_async_copy(dec_hbm, dec_v, load_sem.at[0])
    load_cap = pltpu.make_async_copy(cap_hbm, cap_v, load_sem.at[1])
    load_dec.start()

    barrier = pltpu.get_barrier_semaphore()
    for d in range(1, n):
        pl.semaphore_signal(barrier, inc=1, device_id={"tok": lax.rem(me + d, n)}, device_id_type=MESH)

    @pl.when(has_low)
    def _():
        pl.semaphore_signal(barrier, inc=1, device_id={"lat": low}, device_id_type=MESH)

    @pl.when(has_high)
    def _():
        pl.semaphore_signal(barrier, inc=1, device_id={"lat": high}, device_id_type=MESH)

    pl.semaphore_wait(barrier, n - 1 + has_low.astype(jnp.int32) + has_high.astype(jnp.int32))

    def share_of(j):
        return rows_of(j, share)

    def scatter(src, dst, send, recv, all_spans, i, d):
        lo, hi = all_spans[i]
        peer = lax.rem(me + d, n)
        at = i * (n - 1) + d - 1
        return pltpu.make_async_remote_copy(
            src_ref=src.at[lo:hi, share_of(peer)], dst_ref=dst.at[d - 1, lo:hi],
            send_sem=send.at[at], recv_sem=recv.at[at], device_id={"tok": peer}, device_id_type=MESH,
        )

    def gather(buf, send, recv, all_spans, i, d, owner):
        lo, hi = all_spans[i]
        at = i * (n - 1) + d - 1
        part = buf.at[lo:hi, share_of(owner)]
        return pltpu.make_async_remote_copy(
            src_ref=part, dst_ref=part, send_sem=send.at[at], recv_sem=recv.at[at],
            device_id={"tok": lax.rem(me + n - d, n)}, device_id_type=MESH,
        )

    def pre_copy(i, d):
        return scatter(pre_ref, pre_in, pre_send, pre_recv, first_spans, i, d)

    def dc_copy(i, d):
        return scatter(dc_out, dc_in, dc_send, dc_recv, last_spans, i, d)

    def code_copy(i, d, owner):
        return gather(codes_ref, code_send, code_recv, first_spans, i, d, owner)

    def dp_copy(i, d, owner):
        return gather(dpre_ref, dp_send, dp_recv, last_spans, i, d, owner)

    def other(d):
        return lax.rem(me + d, n)

    def activate(i):
        lo, hi = first_spans[i]
        total = pre_ref[lo:hi, share_of(me)].astype(F32)
        for d in range(1, n):
            pre_copy(i, d).wait_recv()
            total = total + pre_in[d - 1, lo:hi].astype(F32)
        v = total + bias_ref[slot, lo:hi]
        soft = jnp.maximum(v, 0.0) + jnp.log1p(jnp.exp(-jnp.abs(v)))
        codes_ref[lo:hi, share_of(me)] = (soft * live_ref[slot, lo:hi]).astype(BF16)
        for d in range(1, n):
            code_copy(i, d, me).start()

    def codes_here(i):
        for d in range(1, n):
            code_copy(i, d, other(d)).wait_recv()

    def slopes(i):
        lo, hi = last_spans[i]
        total = dc_out[lo:hi, share_of(me)].astype(F32)
        for d in range(1, n):
            dc_copy(i, d).wait_recv()
            total = total + dc_in[d - 1, lo:hi].astype(F32)
        rate = 1.0 - jnp.exp(-codes_ref[lo:hi, share_of(me)].astype(F32))
        dpre_ref[lo:hi, share_of(me)] = ((total + PENALTY) * rate).astype(BF16)
        for d in range(1, n):
            dp_copy(i, d, me).start()

    for d in range(1, n):
        pre_copy(0, d).start()
    activate(0)
    for i in range(1, len(first_spans)):
        for d in range(1, n):
            pre_copy(i, d).start()
    load_dec.wait()
    load_cap.start()
    codes_here(0)

    def chunk_rows(c):
        return rows_of(c, chunk)

    def line_copy(src, dst, send, recv, c, dev):
        return pltpu.make_async_remote_copy(
            src_ref=src.at[chunk_rows(c)], dst_ref=dst.at[chunk_rows(c)], send_sem=send.at[c], recv_sem=recv.at[c],
            device_id={"lat": dev}, device_id_type=MESH,
        )

    def up(c):
        return line_copy(up_out, up_in, up_send, up_recv, c, high)

    def up_first(c):
        return line_copy(part_v, up_in, up_send, up_recv, c, high)

    def down(c):
        return line_copy(down_out, down_in, down_send, down_recv, c, low)

    def down_first(c):
        return line_copy(part_v, down_in, down_send, down_recv, c, low)

    def dec_tile(b):
        return jnp.concatenate([dec_v[ids[k, b]] for k in range(KS)], axis=0)

    def make_part(b):
        tiles = [codes_ref[b, pl.ds(k * TB, TB)] for k in range(KS)]
        part_v[rows_of(b, TB)] = dot(jnp.concatenate(tiles, axis=1), dec_tile(b), 1, 0).astype(BF16)

    up_delay = lag * z
    down_delay = lag * (nz - 1 - z)
    first_delay = jnp.minimum(up_delay, down_delay)
    last_delay = jnp.maximum(up_delay, down_delay)

    def step(t, carry):
        cf = t - first_delay
        cu = t - up_delay
        cd = t - down_delay
        cl = t - last_delay
        stage = jnp.maximum(cf, 0) // per
        fresh = jnp.logical_and(cf >= 0, cf < chunks)

        @pl.when(jnp.logical_and(fresh, lax.rem(jnp.maximum(cf, 0), per) == 0))
        def _():
            for i in range(1, len(first_spans)):
                @pl.when(stage == first_spans[i][0])
                def _():
                    codes_here(i)

            make_part(stage)

        for i in range(1, len(first_spans)):
            @pl.when(cf == first_spans[i - 1][1] * per - per // 2 - 1)
            def _():
                activate(i)

        @pl.when(jnp.logical_and(cu >= 0, cu < chunks))
        def _():
            @pl.when(has_low)
            def _():
                up(cu).wait_recv()

                @pl.when(has_high)
                def _():
                    up_out[chunk_rows(cu)] = (
                        up_in[chunk_rows(cu)].astype(F32) + part_v[chunk_rows(cu)].astype(F32)
                    ).astype(BF16)
                    up(cu).start()

            @pl.when(jnp.logical_not(has_low))
            def _():
                up_first(cu).start()

        @pl.when(jnp.logical_and(cd >= 0, cd < chunks))
        def _():
            @pl.when(has_high)
            def _():
                down(cd).wait_recv()

                @pl.when(has_low)
                def _():
                    down_out[chunk_rows(cd)] = (
                        down_in[chunk_rows(cd)].astype(F32) + part_v[chunk_rows(cd)].astype(F32)
                    ).astype(BF16)
                    down(cd).start()

            @pl.when(jnp.logical_not(has_high))
            def _():
                down_first(cd).start()

        @pl.when(cf == 0)
        def _():
            load_cap.wait()

        @pl.when(jnp.logical_and(fresh, lax.rem(jnp.maximum(cf, 0), per) == per // 2))
        def _():
            capt_v[stage] = cap_v[rows_of(stage, TB)].T

        @pl.when(jnp.logical_and(cl >= 0, cl < chunks))
        def _():
            at = chunk_rows(cl)
            here = part_v[at].astype(F32) + dbias_ref[...] - cap_v[at].astype(F32)

            @pl.when(inner)
            def _():
                both = up_in[at].astype(F32) + down_in[at].astype(F32)
                delta_v[at] = (SCALE_ERR * (here + both)).astype(BF16)

            @pl.when(jnp.logical_not(has_low))
            def _():
                delta_v[at] = (SCALE_ERR * (here + down_in[at].astype(F32))).astype(BF16)

            @pl.when(jnp.logical_not(has_high))
            def _():
                delta_v[at] = (SCALE_ERR * (here + up_in[at].astype(F32))).astype(BF16)

            done = cl // per

            @pl.when(lax.rem(cl, per) == per - 1)
            def _():
                value = dot(delta_v[rows_of(done, TB)], dec_tile(done), 1, 1).astype(BF16)
                for k in range(KS):
                    dc_out[done, pl.ds(k * TB, TB)] = value[:, k * LB:(k + 1) * LB]

                for i in range(len(last_spans)):
                    @pl.when(done == last_spans[i][1] - 1)
                    def _():
                        for d in range(1, n):
                            dc_copy(i, d).start()

            for i in range(len(last_spans) - 1):
                @pl.when(cl == last_spans[i][1] * per - 1 + per // 2)
                def _():
                    slopes(i)

        return carry

    lax.fori_loop(0, chunks + lag * (nz - 1), step, 0)

    slopes(len(last_spans) - 1)

    def drain(c, carry):
        @pl.when(has_high)
        def _():
            up(c).wait_send()

        @pl.when(has_low)
        def _():
            down(c).wait_send()

        return carry

    lax.fori_loop(0, chunks, drain, 0)

    for i in range(len(first_spans)):
        for d in range(1, n):
            pre_copy(i, d).wait_send()
            code_copy(i, d, me).wait_send()
    for i in range(len(last_spans)):
        for d in range(1, n):
            dc_copy(i, d).wait_send()
            dp_copy(i, d, me).wait_send()
            dp_copy(i, d, other(d)).wait_recv()


def middle(ids, pre, bias, live, dec_bias, captured, dec_weight, chunk, lag):
    n = lax.axis_size("tok")
    nz = lax.axis_size("lat")
    tokens, features = captured.shape
    blocks, rows, _ = pre.shape
    lat_dev = dec_weight.shape[0]
    chunks = tokens // chunk
    first_spans = spans([0, 1, blocks])
    last_spans = spans([0, max(blocks - 2, 0), max(blocks - 1, 0), blocks])
    whole = pl.BlockSpec(memory_space=VMEM)
    outside = pl.BlockSpec(memory_space=pltpu.HBM)
    sems = lambda count: [pltpu.SemaphoreType.DMA((count,))]
    wide = VMEM((tokens, features), BF16)
    shares = VMEM((n - 1, blocks, rows // n, LB), BF16)
    return pl.pallas_call(
        functools.partial(middle_kernel, n, nz, chunk, lag, first_spans, last_spans),
        out_shape=[
            jax.ShapeDtypeStruct((blocks, rows, LB), BF16),
            jax.ShapeDtypeStruct((blocks, rows, LB), BF16),
            jax.ShapeDtypeStruct((tokens, features), BF16),
            jax.ShapeDtypeStruct((blocks, features, TB), BF16),
        ],
        in_specs=[pl.BlockSpec(memory_space=pltpu.SMEM)] + [whole] * 4 + [outside] * 2,
        out_specs=[whole] * 4,
        scratch_shapes=[wide, VMEM((lat_dev // LB, LB, features), BF16), wide]
        + [wide] * 4 + [shares, VMEM((blocks, rows, LB), BF16), shares]
        + sems(chunks) * 4 + sems((n - 1) * len(first_spans)) * 4 + sems((n - 1) * len(last_spans)) * 4
        + sems(2),
        compiler_params=pltpu.CompilerParams(
            collective_id=0, has_side_effects=True, vmem_limit_bytes=MIDDLE
        ),
        name="middle",
    )(
        ids, pre, bias, live, dec_bias.reshape(1, features), captured,
        dec_weight.reshape(-1, LB, features),
    )


def grads_kernel(
    ids, delta_v, capt_v, codes_ref, dpre_ref, egrad_in, dgrad_in,
    enc_hbm, dec_hbm, out_e, out_d, acc_e, acc_d,
    members, seen, place, spare, enc_sem, dec_sem,
):
    blocks = capt_v.shape[0]
    groups = members.shape[0]

    def enc_copy(src, g):
        return pltpu.make_async_copy(src, enc_hbm.at[:, rows_of(g, LB)], enc_sem.at[g])

    def dec_copy(src, g):
        return pltpu.make_async_copy(src, dec_hbm.at[rows_of(g, LB)], dec_sem.at[g])

    def clear(g, carry):
        members[g] = 0
        seen[g] = 0
        return carry

    def count(b, carry):
        for k in range(KS):
            members[ids[k, b]] += 1
        return carry

    lax.fori_loop(0, groups, clear, 0)
    lax.fori_loop(0, blocks, count, 0)
    spare[0] = 0

    def work(b, carry):
        for k in range(KS):
            g = ids[k, b]
            s = b * KS + k
            total = members[g]
            before = seen[g]
            seen[g] = before + 1

            def enc_tile():
                return dot(capt_v[b], dpre_ref[b, pl.ds(k * TB, TB)], 1, 0)

            def dec_tile():
                return dot(codes_ref[b, pl.ds(k * TB, TB)], delta_v[rows_of(b, TB)], 0, 0)

            @pl.when(total == 1)
            def _():
                out_e[s] = enc_tile().astype(BF16)
                out_d[s] = dec_tile().astype(BF16)

            @pl.when(total > 1)
            def _():
                @pl.when(before == 0)
                def _():
                    at = spare[0]
                    spare[0] = at + 1
                    place[g] = at
                    acc_e[at] = enc_tile()
                    acc_d[at] = dec_tile()

                @pl.when(before > 0)
                def _():
                    at = place[g]
                    e = acc_e[at] + enc_tile()
                    d = acc_d[at] + dec_tile()

                    @pl.when(before + 1 < total)
                    def _():
                        acc_e[at] = e
                        acc_d[at] = d

                    @pl.when(before + 1 == total)
                    def _():
                        out_e[s] = e.astype(BF16)
                        out_d[s] = d.astype(BF16)

            @pl.when(before + 1 == total)
            def _():
                enc_copy(out_e.at[s], g).start()
                dec_copy(out_d.at[s], g).start()

        return carry

    lax.fori_loop(0, blocks, work, 0)

    def finish(g, carry):
        @pl.when(members[g] > 0)
        def _():
            enc_copy(out_e.at[0], g).wait()
            dec_copy(out_d.at[0], g).wait()

        return carry

    lax.fori_loop(0, groups, finish, 0)


def gradients(ids, delta, capt, codes, dpre, egrad, dgrad, groups):
    tokens, features = delta.shape
    blocks = tokens // TB
    slots = blocks * KS
    whole = pl.BlockSpec(memory_space=VMEM)
    outside = pl.BlockSpec(memory_space=pltpu.HBM)
    shared = max(min(slots // 2, groups), 1)
    return pl.pallas_call(
        grads_kernel,
        in_specs=[pl.BlockSpec(memory_space=pltpu.SMEM)] + [whole] * 4 + [outside] * 2,
        out_specs=[outside, outside],
        input_output_aliases={5: 0, 6: 1},
        scratch_shapes=[
            VMEM((slots, features, LB), BF16), VMEM((slots, LB, features), BF16),
            VMEM((shared, features, LB), F32), VMEM((shared, LB, features), F32),
            pltpu.SMEM((groups,), jnp.int32), pltpu.SMEM((groups,), jnp.int32),
            pltpu.SMEM((groups,), jnp.int32), pltpu.SMEM((1,), jnp.int32),
            pltpu.SemaphoreType.DMA((groups,)), pltpu.SemaphoreType.DMA((groups,)),
        ],
        out_shape=[
            jax.ShapeDtypeStruct((features, groups * LB), BF16),
            jax.ShapeDtypeStruct((groups * LB, features), BF16),
        ],
        compiler_params=pltpu.CompilerParams(vmem_limit_bytes=LAST),
        name="gradients",
    )(ids, delta, capt, codes, dpre, egrad, dgrad)


def local(captured, enc_weight, enc_bias, dec_weight, dec_bias, block_ids, block_counts):
    ids = block_ids.transpose(1, 2, 0).reshape(KS, -1)
    counts = block_counts.reshape(-1)
    pre, bias, live, egrad, dgrad = partial_pre(ids, counts, captured, enc_weight, enc_bias)
    codes, dpre, delta, capt = middle(ids, pre, bias, live, dec_bias, captured, dec_weight, CHUNK, LAG)
    return tuple(gradients(ids, delta, capt, codes, dpre, egrad, dgrad, dec_weight.shape[0] // LB))


def solution(mesh):
    in_specs = (
        P(None, "tok"),
        P("tok", "lat"),
        P("lat"),
        P("lat", "tok"),
        P("tok"),
        P(None, "lat", None),
        P(None, "lat"),
    )
    out_specs = (P("tok", "lat"), P("lat", "tok"))
    return jax.shard_map(local, mesh=mesh, in_specs=in_specs, out_specs=out_specs, check_vma=False)
```

```python
import functools

import jax
import jax.numpy as jnp
from jax import lax
from jax.experimental import pallas as pl
from jax.experimental.pallas import tpu as pltpu
from jax.sharding import PartitionSpec as P

TB = 128
LB = 128
KS = 2

SCALE_ERR = 0.0625
PENALTY = 0.05
CHUNK = 16
LAG = 3
F32 = jnp.float32
BF16 = jnp.bfloat16
MESH = pl.DeviceIdType.MESH
VMEM = pltpu.VMEM
BIG = 52 * 1024 * 1024
MIDDLE = 43 * 1024 * 1024
LAST = 36 * 1024 * 1024


def dot(a, b, ca, cb):
    return lax.dot_general(a, b, (((ca,), (cb,)), ((), ())), preferred_element_type=F32)


def rows_of(b, size):
    return pl.ds(pl.multiple_of(b * size, size), size)


def pre_kernel(ids, cap_hbm, enc_hbm, pre_ref, cap_v, tiles_v, cap_sem, tile_sem):
    blocks = pre_ref.shape[0]

    def loads(b):
        copies = [pltpu.make_async_copy(cap_hbm.at[rows_of(b, TB)], cap_v.at[rows_of(b, TB)], cap_sem.at[b])]
        for k in range(KS):
            copies.append(pltpu.make_async_copy(
                enc_hbm.at[:, rows_of(ids[k, b], LB)], tiles_v.at[b, :, pl.ds(k * LB, LB)], tile_sem.at[b * KS + k]
            ))
        return copies

    def begin(b, carry):
        for copy in loads(b):
            copy.start()
        return carry

    def work(b, carry):
        for copy in loads(b):
            copy.wait()
        pre = dot(cap_v[rows_of(b, TB)], tiles_v[b], 1, 0).astype(BF16)
        for k in range(KS):
            pre_ref[b, pl.ds(k * TB, TB)] = pre[:, k * LB:(k + 1) * LB]
        return carry

    lax.fori_loop(0, blocks, begin, 0)
    lax.fori_loop(0, blocks, work, 0)


def partial_pre(ids, captured, enc_weight):
    tokens, features = captured.shape
    blocks = tokens // TB
    whole = pl.BlockSpec(memory_space=VMEM)
    outside = pl.BlockSpec(memory_space=pltpu.HBM)
    scalars = pl.BlockSpec(memory_space=pltpu.SMEM)
    return pl.pallas_call(
        pre_kernel,
        in_specs=[scalars, outside, outside],
        out_specs=whole,
        scratch_shapes=[
            VMEM((tokens, features), BF16), VMEM((blocks, features, KS * LB), BF16),
            pltpu.SemaphoreType.DMA((blocks,)), pltpu.SemaphoreType.DMA((blocks * KS,)),
        ],
        out_shape=jax.ShapeDtypeStruct((blocks, KS * TB, LB), BF16),
        compiler_params=pltpu.CompilerParams(vmem_limit_bytes=BIG),
        name="partial_pre",
    )(ids, captured, enc_weight)


def spans(cuts):
    return [(lo, hi) for lo, hi in zip(cuts[:-1], cuts[1:]) if lo < hi]


def middle_kernel(
    n, nz, chunk, lag, first_spans, last_spans,
    ids, counts, pre_ref, ebias_ref, dbias_ref, cap_hbm, dec_hbm,
    codes_ref, dpre_ref, delta_v, capt_v,
    bias_ref, live_ref, cap_v, dec_v, part_v, up_in, down_in, up_out, down_out,
    pre_in, dc_out, dc_in,
    up_send, up_recv, down_send, down_recv,
    pre_send, pre_recv, code_send, code_recv, dc_send, dc_recv, dp_send, dp_recv,
    load_sem,
):
    me = lax.axis_index("tok")
    z = lax.axis_index("lat")
    blocks, rows = pre_ref.shape[0], pre_ref.shape[1]
    share = rows // n
    slot = me * share // TB
    per = TB // chunk
    chunks = blocks * per
    has_low = z > 0
    has_high = z < nz - 1
    inner = jnp.logical_and(has_low, has_high)
    low = jnp.maximum(z - 1, 0)
    high = jnp.minimum(z + 1, nz - 1)

    load_dec = pltpu.make_async_copy(dec_hbm, dec_v, load_sem.at[0])
    load_cap = pltpu.make_async_copy(cap_hbm, cap_v, load_sem.at[1])
    load_dec.start()

    barrier = pltpu.get_barrier_semaphore()
    for d in range(1, n):
        pl.semaphore_signal(barrier, inc=1, device_id={"tok": lax.rem(me + d, n)}, device_id_type=MESH)

    @pl.when(has_low)
    def _():
        pl.semaphore_signal(barrier, inc=1, device_id={"lat": low}, device_id_type=MESH)

    @pl.when(has_high)
    def _():
        pl.semaphore_signal(barrier, inc=1, device_id={"lat": high}, device_id_type=MESH)

    def select(b, carry):
        bias_ref[b] = ebias_ref[ids[slot, b]]
        live_ref[b] = jnp.full((1, LB), (slot < counts[b]).astype(F32), F32)
        return carry

    lax.fori_loop(0, blocks, select, 0)
    pl.semaphore_wait(barrier, n - 1 + has_low.astype(jnp.int32) + has_high.astype(jnp.int32))

    def share_of(j):
        return rows_of(j, share)

    def scatter(src, dst, send, recv, all_spans, i, d):
        lo, hi = all_spans[i]
        peer = lax.rem(me + d, n)
        at = i * (n - 1) + d - 1
        return pltpu.make_async_remote_copy(
            src_ref=src.at[lo:hi, share_of(peer)], dst_ref=dst.at[d - 1, lo:hi],
            send_sem=send.at[at], recv_sem=recv.at[at], device_id={"tok": peer}, device_id_type=MESH,
        )

    def gather(buf, send, recv, all_spans, i, d, owner):
        lo, hi = all_spans[i]
        at = i * (n - 1) + d - 1
        part = buf.at[lo:hi, share_of(owner)]
        return pltpu.make_async_remote_copy(
            src_ref=part, dst_ref=part, send_sem=send.at[at], recv_sem=recv.at[at],
            device_id={"tok": lax.rem(me + n - d, n)}, device_id_type=MESH,
        )

    def pre_copy(i, d):
        return scatter(pre_ref, pre_in, pre_send, pre_recv, first_spans, i, d)

    def dc_copy(i, d):
        return scatter(dc_out, dc_in, dc_send, dc_recv, last_spans, i, d)

    def code_copy(i, d, owner):
        return gather(codes_ref, code_send, code_recv, first_spans, i, d, owner)

    def dp_copy(i, d, owner):
        return gather(dpre_ref, dp_send, dp_recv, last_spans, i, d, owner)

    def other(d):
        return lax.rem(me + d, n)

    def activate(i):
        lo, hi = first_spans[i]
        total = pre_ref[lo:hi, share_of(me)].astype(F32)
        for d in range(1, n):
            pre_copy(i, d).wait_recv()
            total = total + pre_in[d - 1, lo:hi].astype(F32)
        v = total + bias_ref[lo:hi]
        soft = jnp.maximum(v, 0.0) + jnp.log1p(jnp.exp(-jnp.abs(v)))
        codes_ref[lo:hi, share_of(me)] = (soft * live_ref[lo:hi]).astype(BF16)
        for d in range(1, n):
            code_copy(i, d, me).start()

    def codes_here(i):
        for d in range(1, n):
            code_copy(i, d, other(d)).wait_recv()

    def slopes(i):
        lo, hi = last_spans[i]
        total = dc_out[lo:hi, share_of(me)].astype(F32)
        for d in range(1, n):
            dc_copy(i, d).wait_recv()
            total = total + dc_in[d - 1, lo:hi].astype(F32)
        rate = 1.0 - jnp.exp(-codes_ref[lo:hi, share_of(me)].astype(F32))
        dpre_ref[lo:hi, share_of(me)] = ((total + PENALTY) * rate).astype(BF16)
        for d in range(1, n):
            dp_copy(i, d, me).start()

    for d in range(1, n):
        pre_copy(0, d).start()
    activate(0)
    for i in range(1, len(first_spans)):
        for d in range(1, n):
            pre_copy(i, d).start()
    load_dec.wait()
    load_cap.start()
    codes_here(0)

    def chunk_rows(c):
        return rows_of(c, chunk)

    def line_copy(src, dst, send, recv, c, dev):
        return pltpu.make_async_remote_copy(
            src_ref=src.at[chunk_rows(c)], dst_ref=dst.at[chunk_rows(c)], send_sem=send.at[c], recv_sem=recv.at[c],
            device_id={"lat": dev}, device_id_type=MESH,
        )

    def up(c):
        return line_copy(up_out, up_in, up_send, up_recv, c, high)

    def up_first(c):
        return line_copy(part_v, up_in, up_send, up_recv, c, high)

    def down(c):
        return line_copy(down_out, down_in, down_send, down_recv, c, low)

    def down_first(c):
        return line_copy(part_v, down_in, down_send, down_recv, c, low)

    def dec_tile(b):
        return jnp.concatenate([dec_v[ids[k, b]] for k in range(KS)], axis=0)

    def make_part(b):
        tiles = [codes_ref[b, pl.ds(k * TB, TB)] for k in range(KS)]
        part_v[rows_of(b, TB)] = dot(jnp.concatenate(tiles, axis=1), dec_tile(b), 1, 0).astype(BF16)

    lower = 2 * z < nz
    up_delay = lag * z
    down_delay = lag * (nz - 1 - z)
    first_delay = jnp.minimum(up_delay, down_delay)
    last_delay = jnp.maximum(up_delay, down_delay)

    def step(t, carry):
        cf = t - first_delay
        cu = t - up_delay
        cd = t - down_delay
        cl = t - last_delay
        stage = jnp.maximum(cf, 0) // per
        fresh = jnp.logical_and(cf >= 0, cf < chunks)

        @pl.when(jnp.logical_and(fresh, lax.rem(jnp.maximum(cf, 0), per) == 0))
        def _():
            for i in range(1, len(first_spans)):
                @pl.when(stage == first_spans[i][0])
                def _():
                    codes_here(i)

            make_part(stage)

        for i in range(1, len(first_spans)):
            @pl.when(cf == first_spans[i - 1][1] * per - per // 2 - 1)
            def _():
                activate(i)

        def pass_up():
            @pl.when(jnp.logical_and(cu >= 0, cu < chunks))
            def _():
                @pl.when(has_low)
                def _():
                    up(cu).wait_recv()

                    @pl.when(has_high)
                    def _():
                        up_out[chunk_rows(cu)] = (
                            up_in[chunk_rows(cu)].astype(F32) + part_v[chunk_rows(cu)].astype(F32)
                        ).astype(BF16)
                        up(cu).start()

                @pl.when(jnp.logical_not(has_low))
                def _():
                    up_first(cu).start()

        pl.when(lower)(pass_up)

        @pl.when(jnp.logical_and(cd >= 0, cd < chunks))
        def _():
            @pl.when(has_high)
            def _():
                down(cd).wait_recv()

                @pl.when(has_low)
                def _():
                    down_out[chunk_rows(cd)] = (
                        down_in[chunk_rows(cd)].astype(F32) + part_v[chunk_rows(cd)].astype(F32)
                    ).astype(BF16)
                    down(cd).start()

            @pl.when(jnp.logical_not(has_high))
            def _():
                down_first(cd).start()

        pl.when(jnp.logical_not(lower))(pass_up)

        @pl.when(cf == 0)
        def _():
            load_cap.wait()

        @pl.when(jnp.logical_and(fresh, lax.rem(jnp.maximum(cf, 0), per) == per // 2))
        def _():
            capt_v[stage] = cap_v[rows_of(stage, TB)].T

        @pl.when(jnp.logical_and(cl >= 0, cl < chunks))
        def _():
            at = chunk_rows(cl)
            here = part_v[at].astype(F32) + dbias_ref[...] - cap_v[at].astype(F32)

            @pl.when(inner)
            def _():
                both = up_in[at].astype(F32) + down_in[at].astype(F32)
                delta_v[at] = (SCALE_ERR * (here + both)).astype(BF16)

            @pl.when(jnp.logical_not(has_low))
            def _():
                delta_v[at] = (SCALE_ERR * (here + down_in[at].astype(F32))).astype(BF16)

            @pl.when(jnp.logical_not(has_high))
            def _():
                delta_v[at] = (SCALE_ERR * (here + up_in[at].astype(F32))).astype(BF16)

            done = cl // per

            @pl.when(lax.rem(cl, per) == per - 1)
            def _():
                value = dot(delta_v[rows_of(done, TB)], dec_tile(done), 1, 1).astype(BF16)
                for k in range(KS):
                    dc_out[done, pl.ds(k * TB, TB)] = value[:, k * LB:(k + 1) * LB]

                for i in range(len(last_spans)):
                    @pl.when(done == last_spans[i][1] - 1)
                    def _():
                        for d in range(1, n):
                            dc_copy(i, d).start()

            for i in range(len(last_spans) - 1):
                @pl.when(cl == last_spans[i][1] * per - 1 + per // 2)
                def _():
                    slopes(i)

        return carry

    lax.fori_loop(0, chunks + lag * (nz - 1), step, 0)

    slopes(len(last_spans) - 1)

    def drain(c, carry):
        @pl.when(has_high)
        def _():
            up(c).wait_send()

        @pl.when(has_low)
        def _():
            down(c).wait_send()

        return carry

    lax.fori_loop(0, chunks, drain, 0)

    for i in range(len(first_spans)):
        for d in range(1, n):
            pre_copy(i, d).wait_send()
            code_copy(i, d, me).wait_send()
    for i in range(len(last_spans)):
        for d in range(1, n):
            dc_copy(i, d).wait_send()
            dp_copy(i, d, me).wait_send()
            dp_copy(i, d, other(d)).wait_recv()


def middle(ids, counts, pre, enc_bias, dec_bias, captured, dec_weight, chunk, lag):
    n = lax.axis_size("tok")
    nz = lax.axis_size("lat")
    tokens, features = captured.shape
    blocks, rows, _ = pre.shape
    lat_dev = dec_weight.shape[0]
    chunks = tokens // chunk
    first_spans = spans([0, 1, blocks])
    last_spans = spans([0, max(blocks - 2, 0), max(blocks - 1, 0), blocks])
    whole = pl.BlockSpec(memory_space=VMEM)
    outside = pl.BlockSpec(memory_space=pltpu.HBM)
    sems = lambda count: [pltpu.SemaphoreType.DMA((count,))]
    wide = VMEM((tokens, features), BF16)
    shares = VMEM((n - 1, blocks, rows // n, LB), BF16)
    return pl.pallas_call(
        functools.partial(middle_kernel, n, nz, chunk, lag, first_spans, last_spans),
        out_shape=[
            jax.ShapeDtypeStruct((blocks, rows, LB), BF16),
            jax.ShapeDtypeStruct((blocks, rows, LB), BF16),
            jax.ShapeDtypeStruct((tokens, features), BF16),
            jax.ShapeDtypeStruct((blocks, features, TB), BF16),
        ],
        in_specs=[pl.BlockSpec(memory_space=pltpu.SMEM)] * 2 + [whole] * 3 + [outside] * 2,
        out_specs=[whole] * 4,
        scratch_shapes=[VMEM((blocks, 1, LB), F32)] * 2 + [wide, VMEM((lat_dev // LB, LB, features), BF16), wide]
        + [wide] * 4 + [shares, VMEM((blocks, rows, LB), BF16), shares]
        + sems(chunks) * 4 + sems((n - 1) * len(first_spans)) * 4 + sems((n - 1) * len(last_spans)) * 4
        + sems(2),
        compiler_params=pltpu.CompilerParams(
            collective_id=0, has_side_effects=True, vmem_limit_bytes=MIDDLE
        ),
        name="middle",
    )(
        ids, counts, pre, enc_bias.reshape(-1, 1, LB), dec_bias.reshape(1, features), captured,
        dec_weight.reshape(-1, LB, features),
    )


def grads_kernel(
    ids, delta_v, capt_v, codes_ref, dpre_ref,
    enc_hbm, dec_hbm, zero_e, zero_d, out_e, out_d, acc_e, acc_d,
    members, seen, place, spare, enc_sem, dec_sem,
):
    blocks = capt_v.shape[0]
    groups = members.shape[0]

    def enc_copy(src, g):
        return pltpu.make_async_copy(src, enc_hbm.at[:, rows_of(g, LB)], enc_sem.at[g])

    def dec_copy(src, g):
        return pltpu.make_async_copy(src, dec_hbm.at[rows_of(g, LB)], dec_sem.at[g])

    def clear(g, carry):
        members[g] = 0
        seen[g] = 0
        return carry

    def count(b, carry):
        for k in range(KS):
            members[ids[k, b]] += 1
        return carry

    def blank(g, carry):
        @pl.when(members[g] == 0)
        def _():
            enc_copy(zero_e, g).start()
            dec_copy(zero_d, g).start()

        return carry

    zero_e[...] = jnp.zeros(zero_e.shape, BF16)
    zero_d[...] = jnp.zeros(zero_d.shape, BF16)
    lax.fori_loop(0, groups, clear, 0)
    lax.fori_loop(0, blocks, count, 0)
    lax.fori_loop(0, groups, blank, 0)
    spare[0] = 0

    def work(b, carry):
        for k in range(KS):
            g = ids[k, b]
            s = b * KS + k
            total = members[g]
            before = seen[g]
            seen[g] = before + 1

            def enc_tile():
                return dot(capt_v[b], dpre_ref[b, pl.ds(k * TB, TB)], 1, 0)

            def dec_tile():
                return dot(codes_ref[b, pl.ds(k * TB, TB)], delta_v[rows_of(b, TB)], 0, 0)

            @pl.when(total == 1)
            def _():
                out_e[s] = enc_tile().astype(BF16)
                out_d[s] = dec_tile().astype(BF16)

            @pl.when(total > 1)
            def _():
                @pl.when(before == 0)
                def _():
                    at = spare[0]
                    spare[0] = at + 1
                    place[g] = at
                    acc_e[at] = enc_tile()
                    acc_d[at] = dec_tile()

                @pl.when(before > 0)
                def _():
                    at = place[g]
                    e = acc_e[at] + enc_tile()
                    d = acc_d[at] + dec_tile()

                    @pl.when(before + 1 < total)
                    def _():
                        acc_e[at] = e
                        acc_d[at] = d

                    @pl.when(before + 1 == total)
                    def _():
                        out_e[s] = e.astype(BF16)
                        out_d[s] = d.astype(BF16)

            @pl.when(before + 1 == total)
            def _():
                enc_copy(out_e.at[s], g).start()
                dec_copy(out_d.at[s], g).start()

        return carry

    lax.fori_loop(0, blocks, work, 0)

    def finish(g, carry):
        enc_copy(zero_e, g).wait()
        dec_copy(zero_d, g).wait()
        return carry

    lax.fori_loop(0, groups, finish, 0)


def gradients(ids, delta, capt, codes, dpre, groups):
    tokens, features = delta.shape
    blocks = tokens // TB
    slots = blocks * KS
    whole = pl.BlockSpec(memory_space=VMEM)
    outside = pl.BlockSpec(memory_space=pltpu.HBM)
    shared = max(min(slots // 2, groups), 1)
    return pl.pallas_call(
        grads_kernel,
        in_specs=[pl.BlockSpec(memory_space=pltpu.SMEM)] + [whole] * 4,
        out_specs=[outside, outside],
        scratch_shapes=[
            VMEM((features, LB), BF16), VMEM((LB, features), BF16),
            VMEM((slots, features, LB), BF16), VMEM((slots, LB, features), BF16),
            VMEM((shared, features, LB), F32), VMEM((shared, LB, features), F32),
            pltpu.SMEM((groups,), jnp.int32), pltpu.SMEM((groups,), jnp.int32),
            pltpu.SMEM((groups,), jnp.int32), pltpu.SMEM((1,), jnp.int32),
            pltpu.SemaphoreType.DMA((groups,)), pltpu.SemaphoreType.DMA((groups,)),
        ],
        out_shape=[
            jax.ShapeDtypeStruct((features, groups * LB), BF16),
            jax.ShapeDtypeStruct((groups * LB, features), BF16),
        ],
        compiler_params=pltpu.CompilerParams(vmem_limit_bytes=LAST),
        name="gradients",
    )(ids, delta, capt, codes, dpre)


def local(captured, enc_weight, enc_bias, dec_weight, dec_bias, block_ids, block_counts):
    ids = block_ids.transpose(1, 2, 0).reshape(KS, -1)
    counts = block_counts.reshape(-1)
    pre = partial_pre(ids, captured, enc_weight)
    codes, dpre, delta, capt = middle(ids, counts, pre, enc_bias, dec_bias, captured, dec_weight, CHUNK, LAG)
    return tuple(gradients(ids, delta, capt, codes, dpre, dec_weight.shape[0] // LB))


def solution(mesh):
    in_specs = (
        P(None, "tok"),
        P("tok", "lat"),
        P("lat"),
        P("lat", "tok"),
        P("tok"),
        P(None, "lat", None),
        P(None, "lat"),
    )
    out_specs = (P("tok", "lat"), P("lat", "tok"))
    return jax.shard_map(local, mesh=mesh, in_specs=in_specs, out_specs=out_specs, check_vma=False)
```
